1024 devices in a mesh: grp: 8 (over x, core), dev: 128 (over z, y).
Axes of the slice: x: 4, y: 4, z: 32, core: 2. Of those that a mesh axis runs over, the one named last changes fastest.
Arguments:
- node_latent: bfloat16 [1024, 128, 256], P(('grp', 'dev')), may hold values from -6 to 6
- edge_latent: bfloat16 [1024, 384, 256], P(('grp', 'dev')), may hold values from -6 to 6
- cut_latent: bfloat16 [1024, 5, 64, 256], P(('grp', 'dev')), may hold values from -6 to 6
- node_cotangent: bfloat16 [1024, 128, 256], P(('grp', 'dev')), may hold values from -6 to 6
- edge_sender: int32 [1024, 384], P(('grp', 'dev')), may hold values from 0 to 127, as said below
- edge_receiver: int32 [1024, 384], P(('grp', 'dev')), may hold values from 0 to 127, as said below
- boundary_rows: int32 [1024, 5, 16], P(('grp', 'dev')), may hold values from 0 to 127, as said below
- cut_slot: int32 [1024, 5, 64], P(('grp', 'dev')), may hold values from 0 to 15
- cut_receiver: int32 [1024, 5, 64], P(('grp', 'dev')), may hold values from 0 to 127, as said below
- node_count: int32 [1024], P(('grp', 'dev')), may hold values from 64 to 128, as said below
- edge_count: int32 [1024], P(('grp', 'dev')), may hold values from 192 to 384, as said below
- edge_first: bfloat16 [768, 256], replicated, may hold values from -0.21875 to 0.21875
- edge_second: bfloat16 [256, 256], replicated, may hold values from -0.375 to 0.375
- edge_gain: float32 [256], replicated, may hold values from 0.1 to 1.9
- node_first: bfloat16 [512, 256], replicated, may hold values from -0.25 to 0.25
- node_second: bfloat16 [256, 256], replicated, may hold values from -0.375 to 0.375
- node_gain: float32 [256], replicated, may hold values from 0.1 to 1.9
Outputs:
- updated_nodes: bfloat16 [1024, 128, 256], P(('grp', 'dev'))
- node_gradient: bfloat16 [1024, 128, 256], P(('grp', 'dev'))
- edge_gradient: bfloat16 [1024, 384, 256], P(('grp', 'dev'))
- cut_gradient: bfloat16 [1024, 5, 64, 256], P(('grp', 'dev'))
The draws below stay inside these ranges and needn't reach their ends.
Inputs may be any that keep to these rules, and one draw needn't show every extreme that they name: Nodes at or beyond a partition's node_count are padding. Inner edges at or beyond a partition's edge_count are padding. `edge_sender`: a node of the partition below its node_count. `edge_receiver`: a node of the partition below its node_count. `boundary_rows`: a node of the partition below its node_count; a node may stand more than once. `cut_receiver`: a node of the partition below its node_count.
All inputs are finite; a program needn't handle non-finite values.
Results may differ from the reference program's by a relative error of at most 0.0095.
Values may be sent and summed in bfloat16 or wider, within the bound.
A program may use at most 32 MiB of HBM per device.

```python
import jax
import jax.numpy as jnp
from jax import lax

L = 256
NODE_DEV = 128
ROUNDS = 5
EDGE_DEV = 384
SEND = 16
CUT = 64
PARTS_SIZE = 1024
N_DEV = 128


def count_table(key, limit, salt):
    counts = jax.random.randint(jax.random.fold_in(key, salt), (PARTS_SIZE,), limit // 2, limit + 1)
    fullest = jax.random.randint(jax.random.fold_in(key, salt + 1), (), 0, PARTS_SIZE)
    counts = jnp.where(jnp.arange(PARTS_SIZE) == fullest, limit, counts)
    return (counts.astype(jnp.int32), fullest)


def local_indices(key, salt, shape):
    counts, fullest = count_table(key, NODE_DEV, 11)
    raw = jax.random.randint(jax.random.fold_in(key, salt), shape, 0, 1 << 20)
    spread = counts.reshape((PARTS_SIZE,) + (1,) * (len(shape) - 1))
    values = raw % spread
    corner = (fullest,) + (0,) * (len(shape) - 1)
    values = values.at[corner].set(NODE_DEV - 1)
    return values.astype(jnp.int32)


def draw_node_count(key, part):
    counts, fullest = count_table(key, NODE_DEV, 11)
    return counts


def draw_edge_count(key, part):
    counts, fullest = count_table(key, EDGE_DEV, 31)
    return counts


def draw_edge_sender(key, part):
    return local_indices(key, 21, (PARTS_SIZE, EDGE_DEV))


def draw_edge_receiver(key, part):
    return local_indices(key, 22, (PARTS_SIZE, EDGE_DEV))


def draw_boundary_rows(key, part):
    return local_indices(key, 23, (PARTS_SIZE, ROUNDS, SEND))


def draw_cut_receiver(key, part):
    return local_indices(key, 24, (PARTS_SIZE, ROUNDS, CUT))


def with_ends(result, own_key, smallest, top_value):
    index_at = [jax.random.randint(jax.random.fold_in(own_key, axis), (), 0, length) for axis, length in enumerate(result.shape)]
    widest = result.shape.index(max(result.shape))
    beside = index_at[:widest] + [(index_at[widest] + 1) % result.shape[widest]] + index_at[widest + 1:]
    return result.at[tuple(index_at)].set(smallest).at[tuple(beside)].set(top_value)


def block_levels(key, shape, cuts, least, high):
    factor_of, own = 1.0, jax.random.fold_in(key, 6)
    for axis_at, blocks in cuts:
        heights = jnp.exp(jax.random.uniform(jax.random.fold_in(own, axis_at), (blocks,), jnp.float32, least / len(cuts), high / len(cuts)))
        factor_of = factor_of * jnp.repeat(heights, shape[axis_at] // blocks).reshape([-1 if axis == axis_at else 1 for axis in range(len(shape))])
    return factor_of


def scatter_about(stream_key, dims, width, bound, split=(), kind=jnp.bfloat16):
    drawn = width * jax.random.normal(stream_key, dims, jnp.float32)
    if split:
        drawn = drawn * block_levels(stream_key, dims, split, -0.22, 0.18)
    return jnp.clip(drawn, -bound, bound).astype(kind)


def setup_inputs(seed: int = 0) -> dict:
    splits = jax.random.split(jax.random.key(seed), 18)
    return {
        "node_latent": scatter_about(splits[0], (PARTS_SIZE, NODE_DEV, L), 1.0, 6.0, ((0, 1024),)),
        "edge_latent": scatter_about(splits[1], (PARTS_SIZE, EDGE_DEV, L), 1.0, 6.0, ((0, 1024),)),
        "cut_latent": scatter_about(splits[2], (PARTS_SIZE, ROUNDS, CUT, L), 1.0, 6.0, ((0, 1024),)),
        "node_cotangent": scatter_about(splits[3], (PARTS_SIZE, NODE_DEV, L), 1.0, 6.0, ((0, 1024),)),
        "edge_sender": draw_edge_sender(jax.random.fold_in(splits[17], 71), 0),
        "edge_receiver": draw_edge_receiver(jax.random.fold_in(splits[17], 71), 0),
        "boundary_rows": draw_boundary_rows(jax.random.fold_in(splits[17], 71), 0),
        "cut_slot": with_ends(jax.random.randint(splits[7], (PARTS_SIZE, ROUNDS, CUT), 0, SEND), jax.random.fold_in(splits[7], 1), 0, SEND - 1).astype(jnp.int32),
        "cut_receiver": draw_cut_receiver(jax.random.fold_in(splits[17], 71), 0),
        "node_count": draw_node_count(jax.random.fold_in(splits[17], 71), 0),
        "edge_count": draw_edge_count(jax.random.fold_in(splits[17], 71), 0),
        "edge_first": scatter_about(splits[11], (3 * L, L), (3 * L) ** -0.5, 0.21875),
        "edge_second": scatter_about(splits[12], (L, L), L ** -0.5, 0.375),
        "edge_gain": jnp.clip(1.0 + 0.18 * jax.random.normal(splits[13], (L,), jnp.float32), 0.1, 1.9),
        "node_first": scatter_about(splits[14], (2 * L, L), (2 * L) ** -0.5, 0.25),
        "node_second": scatter_about(splits[15], (L, L), L ** -0.5, 0.375),
        "node_gain": jnp.clip(1.0 + 0.18 * jax.random.normal(splits[16], (L,), jnp.float32), 0.1, 1.9),
    }


epsilon = 1e-05

def layer_norm(values, gain):
    centre = lax.optimization_barrier(jnp.mean(values, axis=-1, keepdims=True))
    centred = values - centre
    variance = lax.optimization_barrier(jnp.mean(centred * centred, axis=-1, keepdims=True))
    inverse = 1.0 / jnp.sqrt(variance + epsilon)
    normed = centred * inverse
    return (normed * gain, normed, inverse)

def norm_backward(upstream, gain, normed, inverse):
    scaled = upstream * gain
    first_mean = lax.optimization_barrier(jnp.mean(scaled, axis=-1, keepdims=True))
    second_mean = lax.optimization_barrier(jnp.mean(scaled * normed, axis=-1, keepdims=True))
    return inverse * (scaled - first_mean - normed * second_mean)

def silu_slope(values):
    sigmoid = jax.nn.sigmoid(values)
    return sigmoid * (1.0 + values * (1.0 - sigmoid))

def partner_of(parts, round_index):
    if round_index < 2:
        return jnp.bitwise_xor(parts, N_DEV * 2 ** round_index)
    return jnp.bitwise_xor(parts, 2 ** (round_index - 2))

def pick_rows(table, indices):
    return table[indices]

def local_pass(inputs, weights):
    nodes, edges, cut_edges, cotangent, senders, receivers_local, slots, cut_targets, count_nodes, count_edges, incoming = inputs
    edge_first, edge_second, edge_gain, node_first, node_second, node_gain = weights
    valid = (jnp.arange(NODE_DEV) < count_nodes).astype(jnp.float32)[:, None]
    used = (jnp.arange(EDGE_DEV) < count_edges).astype(jnp.float32)
    cut_flat = cut_targets.reshape(-1)
    sender_rows = jax.vmap(pick_rows)(incoming, slots).reshape(-1, L)
    local_input = jnp.concatenate([nodes[receivers_local], nodes[senders], edges], 1)
    cut_input = jnp.concatenate([nodes[cut_flat], sender_rows, cut_edges.reshape(-1, L)], 1)
    edge_input = jnp.concatenate([local_input, cut_input], 0)
    receivers = jnp.concatenate([receivers_local, cut_flat])
    mask = jnp.concatenate([used, jnp.ones((cut_flat.shape[0],), jnp.float32)])[:, None]
    pre_edge = jnp.dot(edge_input, edge_first, preferred_element_type=jnp.float32)
    act_edge = jax.nn.silu(pre_edge).astype(jnp.bfloat16)
    out_edge = jnp.dot(act_edge, edge_second, preferred_element_type=jnp.float32)
    normed_edge, edge_normed, edge_inverse = layer_norm(out_edge, edge_gain)
    message = normed_edge * mask
    received_sum = jnp.zeros((NODE_DEV, L), jnp.float32).at[receivers].add(message)
    node_input = jnp.concatenate([nodes, received_sum.astype(jnp.bfloat16)], 1)
    pre_node = jnp.dot(node_input, node_first, preferred_element_type=jnp.float32)
    act_node = jax.nn.silu(pre_node).astype(jnp.bfloat16)
    out_node = jnp.dot(act_node, node_second, preferred_element_type=jnp.float32)
    normed_node, node_normed, node_inverse = layer_norm(out_node, node_gain)
    updated = ((nodes.astype(jnp.float32) + normed_node) * valid).astype(jnp.bfloat16)
    masked_cotangent = cotangent.astype(jnp.float32) * valid
    grad_out_node = norm_backward(masked_cotangent, node_gain, node_normed, node_inverse).astype(jnp.bfloat16)
    grad_act_node = jnp.dot(grad_out_node, node_second.T, preferred_element_type=jnp.float32)
    grad_pre_node = (grad_act_node * silu_slope(pre_node)).astype(jnp.bfloat16)
    grad_node_input = jnp.dot(grad_pre_node, node_first.T, preferred_element_type=jnp.float32)
    grad_message = grad_node_input[:, L:][receivers] * mask
    grad_out_edge = norm_backward(grad_message, edge_gain, edge_normed, edge_inverse).astype(jnp.bfloat16)
    grad_act_edge = jnp.dot(grad_out_edge, edge_second.T, preferred_element_type=jnp.float32)
    grad_pre_edge = (grad_act_edge * silu_slope(pre_edge)).astype(jnp.bfloat16)
    grad_edge_input = jnp.dot(grad_pre_edge, edge_first.T, preferred_element_type=jnp.float32)
    gradient = masked_cotangent + grad_node_input[:, :L]
    gradient = gradient.at[receivers].add(grad_edge_input[:, :L])
    gradient = gradient.at[senders].add(grad_edge_input[:EDGE_DEV, L:2 * L])
    edge_gradient = grad_edge_input[:EDGE_DEV, 2 * L:].astype(jnp.bfloat16)
    cut_gradient = grad_edge_input[EDGE_DEV:, 2 * L:].reshape(ROUNDS, CUT, L).astype(jnp.bfloat16)
    sender_part = grad_edge_input[EDGE_DEV:, L:2 * L].reshape(ROUNDS, CUT, L)

    def slot_sum(slot_ids, values):
        return jnp.zeros((SEND, L), jnp.float32).at[slot_ids].add(values)
    slot_sums = jax.vmap(slot_sum)(slots, sender_part)
    return (updated, gradient, edge_gradient, cut_gradient, slot_sums)

def add_rows(gradient, rows, values):
    return gradient.at[rows].add(values)

def reference(node_latent, edge_latent, cut_latent, node_cotangent, edge_sender, edge_receiver, boundary_rows, cut_slot, cut_receiver, node_count, edge_count, edge_first, edge_second, edge_gain, node_first, node_second, node_gain):
    parts = jnp.arange(PARTS_SIZE, dtype=jnp.int32)
    partners = [partner_of(parts, round_index) for round_index in range(ROUNDS)]
    sent = jax.vmap(pick_rows)(node_latent, boundary_rows)
    incoming = jnp.stack([sent[partners[round_index], round_index] for round_index in range(ROUNDS)], 1)
    weights = (edge_first, edge_second, edge_gain, node_first, node_second, node_gain)

    def one_part(inputs):
        return local_pass(inputs, weights)
    updated, gradient, edge_gradient, cut_gradient, slot_sums = lax.map(one_part, (node_latent, edge_latent, cut_latent, node_cotangent, edge_sender, edge_receiver, cut_slot, cut_receiver, node_count, edge_count, incoming))
    for round_index in range(ROUNDS):
        returned = slot_sums[partners[round_index], round_index]
        gradient = jax.vmap(add_rows)(gradient, boundary_rows[:, round_index], returned)
    return (updated, gradient.astype(jnp.bfloat16), edge_gradient, cut_gradient)
```

```python
import jax
import jax.numpy as jnp
from jax import lax
from jax.experimental import pallas as pl
from jax.experimental.pallas import tpu as pltpu
from jax.sharding import PartitionSpec as P

F32 = jnp.float32
BF16 = jnp.bfloat16
MESH = pl.DeviceIdType.MESH
EPS = 1e-5

N = 128
L = 256
E = 384
R = 5
C = 64
S = 16
CUTS = R * C
ROWS = E + CUTS


def dot(a, b):
    return jnp.dot(a, b, preferred_element_type=F32)


def dot_nt(a, b):
    return lax.dot_general(a, b, (((1,), (1,)), ((), ())), preferred_element_type=F32)


def dot_tn(a, b):
    return lax.dot_general(a, b, (((0,), (0,)), ((), ())), preferred_element_type=F32)


def flip(index, bit):
    step = 1 << bit
    return index + step - 2 * step * lax.rem(lax.div(index, step), 2)


def column(rows_of, count, width):
    wide = jnp.concatenate([jnp.broadcast_to(rows_of(i), (width, width)) for i in range(count)], 0)
    total = count * width
    at = lax.broadcasted_iota(jnp.int32, (total, width), 0)
    lane = lax.broadcasted_iota(jnp.int32, (total, width), 1)
    keep = lax.rem(at, width) == lane
    return jnp.sum(jnp.where(keep, wide.astype(F32), 0.0), axis=1, keepdims=True)


def one_hot(col, width=N):
    lane = lax.broadcasted_iota(jnp.int32, (col.shape[0], width), 1).astype(F32)
    return (col == lane).astype(F32).astype(BF16)


def silu_pair(v):
    s = 0.5 * jnp.tanh(0.5 * v) + 0.5
    act = v * s
    return act, s + act * (1.0 - s)


def normed(y):
    mean = jnp.mean(y, axis=-1, keepdims=True)
    cent = y - mean
    var = jnp.mean(cent * cent, axis=-1, keepdims=True)
    inv = lax.rsqrt(var + EPS)
    return cent * inv, inv


def norm_back(d, xhat, inv):
    m1 = jnp.mean(d, axis=-1, keepdims=True)
    m2 = jnp.mean(d * xhat, axis=-1, keepdims=True)
    return inv * (d - m1 - xhat * m2)


def kernel(
    nodes_h, edges_h, cut_h, cot_h, send_h, recv_h, bound_h, slot_h, crecv_h, ncount_h, ecount_h,
    ef_h, es_h, eg_h, nf_h, ns_h, ng_h,
    upd_h, grad_h, egrad_h, cgrad_h,
    nodes, edges, cut, cot, sendi, recvi, bound, slot, crecv, ncount, ecount,
    ef, es, eg, nf, ns, ng,
    upd, grad, egrad, cgrad,
    out_rows, in_rows, out_sums, in_sums, comb, comb_cut, oh, oh2, xhat, inv, slope, gpe,
    in_sem, out_sem, s1, r1, s2, r2,
):
    g = lax.axis_index("grp")
    d = lax.axis_index("dev")
    partners = [
        (flip(g, 0), d), (flip(g, 1), d), (g, flip(d, 0)), (g, flip(d, 1)), (g, flip(d, 2)),
    ]
    barrier = pltpu.get_barrier_semaphore()
    for p in partners:
        pl.semaphore_signal(barrier, inc=1, device_id=p, device_id_type=MESH)

    pairs = [
        (nodes_h, nodes), (bound_h, bound), (recv_h, recvi), (send_h, sendi), (ecount_h, ecount),
        (ef_h, ef), (edges_h, edges), (es_h, es), (crecv_h, crecv), (slot_h, slot), (cut_h, cut),
        (nf_h, nf), (ns_h, ns), (eg_h, eg), (ng_h, ng), (cot_h, cot), (ncount_h, ncount),
    ]
    loads = {}
    for i, (src, dst) in enumerate(pairs):
        c = pltpu.make_async_copy(src, dst, in_sem.at[i])
        c.start()
        loads[id(dst)] = c

    def need(*refs):
        for r in refs:
            loads[id(r)].wait()

    in_rows[R * S:, :] = jnp.zeros((N - R * S, L), BF16)
    in_sums[R * S:, :] = jnp.zeros((N - R * S, L), BF16)

    need(nodes, bound)
    bcol = column(lambda i: bound[i:i + 1, :], R, S)
    ohb = one_hot(bcol)
    out_rows[...] = dot(ohb, nodes[...]).astype(BF16)
    pl.semaphore_wait(barrier, R)
    first = []
    for r, p in enumerate(partners):
        c = pltpu.make_async_remote_copy(
            src_ref=out_rows.at[pl.ds(S * r, S)], dst_ref=in_rows.at[pl.ds(S * r, S)],
            send_sem=s1.at[r], recv_sem=r1.at[r], device_id=p, device_id_type=MESH)
        c.start()
        first.append(c)

    need(recvi, sendi, ecount)
    rcol = column(lambda i: recvi[:, N * i:N * i + N], E // N, N)
    at = lax.broadcasted_iota(jnp.int32, (E, 1), 0)
    rcol = jnp.where(at < ecount[...], rcol, -1.0)
    oh[0:E, :] = one_hot(rcol)
    oh2[0:E, :] = one_hot(column(lambda i: sendi[:, N * i:N * i + N], E // N, N))

    need(ef)
    nr = dot(nodes[...], ef[0:L, :]).astype(BF16)
    comb[0:N, :] = nr
    comb[N:, :] = dot(nodes[...], ef[L:2 * L, :]).astype(BF16)
    comb_cut[0:N, :] = nr
    need(edges, es)

    def forward(start, size, latent, table):
        rows = pl.ds(start, size)
        pick = jnp.concatenate([oh[rows, :], oh2[rows, :]], 1)
        pre = dot(pick, table[...]) + dot(latent, ef[2 * L:, :])
        act, sl = silu_pair(pre)
        slope[rows, :] = sl
        xh, iv = normed(dot(act.astype(BF16), es[...]))
        xhat[rows, :] = xh.astype(BF16)
        inv[rows, :] = iv

    for b in range(E // 128):
        forward(128 * b, 128, edges[128 * b:128 * b + 128, :], comb)

    need(crecv, slot, cut, nf, ns, eg, ng, cot, ncount)
    oh[E:, :] = one_hot(column(lambda i: crecv[i:i + 1, :], R, C))
    rnd = lax.div(lax.broadcasted_iota(jnp.int32, (CUTS, 1), 0), C).astype(F32)
    oh2[E:, :] = one_hot(column(lambda i: slot[i:i + 1, :], R, C) + S * rnd)
    pre_node_own = dot(nodes[...], nf[0:L, :])

    for c in first:
        c.wait_recv()
    comb_cut[N:, :] = dot(in_rows[...], ef[L:2 * L, :]).astype(BF16)
    for b in range(2):
        forward(E + 160 * b, 160, cut[160 * b:160 * b + 160, :], comb_cut)

    received = (dot_tn(oh[...], xhat[...]) * eg[...]).astype(BF16)
    act, sl = silu_pair(pre_node_own + dot(received, nf[L:, :]))
    nx, ninv = normed(dot(act.astype(BF16), ns[...]))
    live = lax.broadcasted_iota(jnp.int32, (N, 1), 0) < ncount[...]
    gain = ng[...]
    upd[...] = jnp.where(live, nodes[...].astype(F32) + nx * gain, 0.0).astype(BF16)
    out0 = pltpu.make_async_copy(upd, upd_h, out_sem.at[0])
    out0.start()
    mcot = jnp.where(live, cot[...].astype(F32), 0.0)
    goo = norm_back(mcot * gain, nx, ninv).astype(BF16)
    gpn = (dot_nt(goo, ns[...]) * sl).astype(BF16)
    base = mcot + dot_nt(gpn, nf[0:L, :])
    gm = (dot_nt(gpn, nf[L:, :]) * eg[...]).astype(BF16)

    def backward(start, size):
        rows = pl.ds(start, size)
        dd = dot(oh[rows, :], gm)
        goe = norm_back(dd, xhat[rows, :].astype(F32), inv[rows, :]).astype(BF16)
        gpe[rows, :] = (dot_nt(goe, es[...]) * slope[rows, :]).astype(BF16)

    for b in range(2):
        backward(E + 160 * b, 160)
    out_sums[...] = dot_tn(oh2[E:, :], gpe[E:, :]).astype(BF16)
    second = []
    for r, p in enumerate(partners):
        c = pltpu.make_async_remote_copy(
            src_ref=out_sums.at[pl.ds(S * r, S)], dst_ref=in_sums.at[pl.ds(S * r, S)],
            send_sem=s2.at[r], recv_sem=r2.at[r], device_id=p, device_id_type=MESH)
        c.start()
        second.append(c)
    cgrad[...] = dot_nt(gpe[E:, :], ef[2 * L:, :]).astype(BF16)
    out3 = pltpu.make_async_copy(cgrad, cgrad_h, out_sem.at[3])
    out3.start()
    for b in range(E // 128):
        backward(128 * b, 128)
    egrad[...] = dot_nt(gpe[0:E, :], ef[2 * L:, :]).astype(BF16)
    out2 = pltpu.make_async_copy(egrad, egrad_h, out_sem.at[2])
    out2.start()
    rsum = dot_tn(oh[...], gpe[...]).astype(BF16)
    base = base + dot_nt(rsum, ef[0:L, :])
    ssum = dot_tn(oh2[0:E, :], gpe[0:E, :])
    for c in second:
        c.wait_recv()
    ssum = (ssum + dot_tn(ohb, in_sums[0:R * S, :])).astype(BF16)
    grad[...] = (base + dot_nt(ssum, ef[L:2 * L, :])).astype(BF16)
    out1 = pltpu.make_async_copy(grad, grad_h, out_sem.at[1])
    out1.start()
    for c in first + second:
        c.wait_send()
    for c in (out0, out1, out2, out3):
        c.wait()


def shards(
    node_latent, edge_latent, cut_latent, node_cotangent, edge_sender, edge_receiver, boundary_rows,
    cut_slot, cut_receiver, node_count, edge_count, edge_first, edge_second, edge_gain, node_first,
    node_second, node_gain,
):
    i32 = jnp.int32
    anyspec = pl.BlockSpec(memory_space=pl.ANY)
    outs = pl.pallas_call(
        kernel,
        out_shape=(
            jax.ShapeDtypeStruct((N, L), BF16),
            jax.ShapeDtypeStruct((N, L), BF16),
            jax.ShapeDtypeStruct((E, L), BF16),
            jax.ShapeDtypeStruct((CUTS, L), BF16),
        ),
        in_specs=[anyspec] * 17,
        out_specs=(anyspec,) * 4,
        scratch_shapes=[
            pltpu.VMEM((N, L), BF16), pltpu.VMEM((E, L), BF16), pltpu.VMEM((CUTS, L), BF16),
            pltpu.VMEM((N, L), BF16), pltpu.VMEM((1, E), i32), pltpu.VMEM((1, E), i32),
            pltpu.VMEM((R, S), i32), pltpu.VMEM((R, C), i32), pltpu.VMEM((R, C), i32),
            pltpu.VMEM((1, 1), i32), pltpu.VMEM((1, 1), i32),
            pltpu.VMEM((3 * L, L), BF16), pltpu.VMEM((L, L), BF16), pltpu.VMEM((1, L), F32),
            pltpu.VMEM((2 * L, L), BF16), pltpu.VMEM((L, L), BF16), pltpu.VMEM((1, L), F32),
            pltpu.VMEM((N, L), BF16), pltpu.VMEM((N, L), BF16), pltpu.VMEM((E, L), BF16),
            pltpu.VMEM((CUTS, L), BF16),
            pltpu.VMEM((R * S, L), BF16), pltpu.VMEM((N, L), BF16),
            pltpu.VMEM((N, L), BF16), pltpu.VMEM((N, L), BF16),
            pltpu.VMEM((2 * N, L), BF16), pltpu.VMEM((2 * N, L), BF16),
            pltpu.VMEM((ROWS, N), BF16), pltpu.VMEM((ROWS, N), BF16),
            pltpu.VMEM((ROWS, L), BF16), pltpu.VMEM((ROWS, 1), F32), pltpu.VMEM((ROWS, L), F32),
            pltpu.VMEM((ROWS, L), BF16),
            pltpu.SemaphoreType.DMA((17,)), pltpu.SemaphoreType.DMA((4,)),
            pltpu.SemaphoreType.DMA((R,)), pltpu.SemaphoreType.DMA((R,)),
            pltpu.SemaphoreType.DMA((R,)), pltpu.SemaphoreType.DMA((R,)),
        ],
        compiler_params=pltpu.CompilerParams(collective_id=0, has_side_effects=True),
        name="message_step",
    )(
        node_latent[0], edge_latent[0], cut_latent[0].reshape(CUTS, L), node_cotangent[0],
        edge_sender, edge_receiver, boundary_rows[0], cut_slot[0], cut_receiver[0],
        node_count.reshape(1, 1), edge_count.reshape(1, 1),
        edge_first, edge_second, edge_gain.reshape(1, L), node_first, node_second,
        node_gain.reshape(1, L),
    )
    updated, gradient, edge_gradient, cut_gradient = outs
    return updated[None], gradient[None], edge_gradient[None], cut_gradient.reshape(1, R, C, L)


def solution(mesh):
    part = ("grp", "dev")
    three = P(part, None, None)
    four = P(part, None, None, None)
    placed = (
        three, three, four, three, P(part, None), P(part, None), three, three, three, P(part),
        P(part), P(), P(), P(), P(), P(), P(),
    )
    return jax.shard_map(
        shards, mesh=mesh, in_specs=placed, out_specs=(three, three, three, four), check_vma=False,
    )
```

```python
import jax
import jax.numpy as jnp
from jax import lax
from jax.experimental import pallas as pl
from jax.experimental.pallas import tpu as pltpu
from jax.sharding import PartitionSpec as P

F32 = jnp.float32
BF16 = jnp.bfloat16
MESH = pl.DeviceIdType.MESH
EPS = 1e-5

N = 128
L = 256
E = 384
R = 5
C = 64
S = 16
CUTS = R * C
ROWS = E + CUTS


def dot(a, b):
    return jnp.dot(a, b, preferred_element_type=F32)


def dot_nt(a, b):
    return lax.dot_general(a, b, (((1,), (1,)), ((), ())), preferred_element_type=F32)


def dot_tn(a, b):
    return lax.dot_general(a, b, (((0,), (0,)), ((), ())), preferred_element_type=F32)


def flip(index, bit):
    step = 1 << bit
    return index + step - 2 * step * lax.rem(lax.div(index, step), 2)


def column(rows_of, count, width):
    wide = jnp.concatenate([jnp.broadcast_to(rows_of(i), (width, width)) for i in range(count)], 0)
    total = count * width
    at = lax.broadcasted_iota(jnp.int32, (total, width), 0)
    lane = lax.broadcasted_iota(jnp.int32, (total, width), 1)
    keep = lax.rem(at, width) == lane
    return jnp.sum(jnp.where(keep, wide.astype(F32), 0.0), axis=1, keepdims=True)


def one_hot(col, width=N):
    lane = lax.broadcasted_iota(jnp.int32, (col.shape[0], width), 1).astype(F32)
    return (col == lane).astype(F32).astype(BF16)


def silu_pair(v):
    s = 0.5 * jnp.tanh(0.5 * v) + 0.5
    act = v * s
    return act, s + act * (1.0 - s)


def normed(y):
    mean = jnp.mean(y, axis=-1, keepdims=True)
    cent = y - mean
    var = jnp.mean(cent * cent, axis=-1, keepdims=True)
    inv = lax.rsqrt(var + EPS)
    return cent * inv, inv


def norm_back(d, xhat, inv):
    m1 = jnp.mean(d, axis=-1, keepdims=True)
    m2 = jnp.mean(d * xhat, axis=-1, keepdims=True)
    return inv * (d - m1 - xhat * m2)


def kernel(
    nodes_h, edges_h, cut_h, cot_h, send_h, recv_h, bound_h, slot_h, crecv_h, ncount_h, ecount_h,
    ef_h, es_h, eg_h, nf_h, ns_h, ng_h,
    upd, grad, egrad, cgrad,
    nodes, edges, cut, cot, sendi, recvi, bound, slot, crecv, ncount, ecount,
    ef, es, eg, nf, ns, ng,
    out_rows, in_rows, out_sums, in_sums, comb, comb_cut, oh, oh2, xhat, inv, slope, gpe,
    in_sem, s1, r1, s2, r2,
):
    g = lax.axis_index("grp")
    d = lax.axis_index("dev")
    partners = [
        (flip(g, 0), d), (flip(g, 1), d), (g, flip(d, 0)), (g, flip(d, 1)), (g, flip(d, 2)),
    ]
    barrier = pltpu.get_barrier_semaphore()
    for p in partners:
        pl.semaphore_signal(barrier, inc=1, device_id=p, device_id_type=MESH)

    pairs = [
        (nodes_h, nodes), (bound_h, bound), (recv_h, recvi), (send_h, sendi), (ecount_h, ecount),
        (ef_h, ef), (edges_h, edges), (es_h, es), (crecv_h, crecv), (slot_h, slot), (cut_h, cut),
        (nf_h, nf), (ns_h, ns), (eg_h, eg), (ng_h, ng), (cot_h, cot), (ncount_h, ncount),
    ]
    loads = {}
    for i, (src, dst) in enumerate(pairs):
        c = pltpu.make_async_copy(src, dst, in_sem.at[i])
        c.start()
        loads[id(dst)] = c

    def need(*refs):
        for r in refs:
            loads[id(r)].wait()

    in_rows[R * S:, :] = jnp.zeros((N - R * S, L), BF16)
    in_sums[R * S:, :] = jnp.zeros((N - R * S, L), BF16)

    need(nodes, bound)
    bcol = column(lambda i: bound[i], R, S)
    ohb = one_hot(bcol)
    out_rows[...] = dot(ohb, nodes[...]).astype(BF16)
    pl.semaphore_wait(barrier, R)
    first = []
    for r, p in enumerate(partners):
        c = pltpu.make_async_remote_copy(
            src_ref=out_rows.at[pl.ds(S * r, S)], dst_ref=in_rows.at[pl.ds(S * r, S)],
            send_sem=s1.at[r], recv_sem=r1.at[r], device_id=p, device_id_type=MESH)
        c.start()
        first.append(c)

    need(recvi, sendi, ecount)
    rcol = column(lambda i: recvi[:, N * i:N * i + N], E // N, N)
    at = lax.broadcasted_iota(jnp.int32, (E, 1), 0)
    rcol = jnp.where(at < ecount[...], rcol, -1.0)
    oh[0:E, :] = one_hot(rcol)
    oh2[0:E, :] = one_hot(column(lambda i: sendi[:, N * i:N * i + N], E // N, N))

    need(ef)
    nr = dot(nodes[...], ef[0:L, :]).astype(BF16)
    comb[0:N, :] = nr
    comb[N:, :] = dot(nodes[...], ef[L:2 * L, :]).astype(BF16)
    comb_cut[0:N, :] = nr
    need(edges, es)

    def forward(start, size, latent, table):
        rows = pl.ds(start, size)
        pick = jnp.concatenate([oh[rows, :], oh2[rows, :]], 1)
        pre = dot(pick, table[...]) + dot(latent, ef[2 * L:, :])
        act, sl = silu_pair(pre)
        slope[rows, :] = sl
        xh, iv = normed(dot(act.astype(BF16), es[...]))
        xhat[rows, :] = xh.astype(BF16)
        inv[rows, :] = iv

    for b in range(E // 128):
        forward(128 * b, 128, edges[128 * b:128 * b + 128, :], comb)

    need(crecv, slot, cut, nf, ns, eg, ng, cot, ncount)
    oh[E:, :] = one_hot(column(lambda i: crecv[i], R, C))
    rnd = lax.div(lax.broadcasted_iota(jnp.int32, (CUTS, 1), 0), C).astype(F32)
    oh2[E:, :] = one_hot(column(lambda i: slot[i], R, C) + S * rnd)
    pre_node_own = dot(nodes[...], nf[0:L, :])

    for c in first:
        c.wait_recv()
    comb_cut[N:, :] = dot(in_rows[...], ef[L:2 * L, :]).astype(BF16)
    for b in range(2):
        forward(E + 160 * b, 160, cut[160 * b:160 * b + 160, :], comb_cut)

    received = (dot_tn(oh[...], xhat[...]) * eg[...]).astype(BF16)
    act, sl = silu_pair(pre_node_own + dot(received, nf[L:, :]))
    nx, ninv = normed(dot(act.astype(BF16), ns[...]))
    live = lax.broadcasted_iota(jnp.int32, (N, 1), 0) < ncount[...]
    gain = ng[...]
    upd[...] = jnp.where(live, nodes[...].astype(F32) + nx * gain, 0.0).astype(BF16)
    mcot = jnp.where(live, cot[...].astype(F32), 0.0)
    goo = norm_back(mcot * gain, nx, ninv).astype(BF16)
    gpn = (dot_nt(goo, ns[...]) * sl).astype(BF16)
    base = mcot + dot_nt(gpn, nf[0:L, :])
    gm = (dot_nt(gpn, nf[L:, :]) * eg[...]).astype(BF16)

    def backward(start, size):
        rows = pl.ds(start, size)
        dd = dot(oh[rows, :], gm)
        goe = norm_back(dd, xhat[rows, :].astype(F32), inv[rows, :]).astype(BF16)
        gpe[rows, :] = (dot_nt(goe, es[...]) * slope[rows, :]).astype(BF16)

    for b in range(2):
        backward(E + 160 * b, 160)
    out_sums[...] = dot_tn(oh2[E:, :], gpe[E:, :]).astype(BF16)
    second = []
    for r, p in enumerate(partners):
        c = pltpu.make_async_remote_copy(
            src_ref=out_sums.at[pl.ds(S * r, S)], dst_ref=in_sums.at[pl.ds(S * r, S)],
            send_sem=s2.at[r], recv_sem=r2.at[r], device_id=p, device_id_type=MESH)
        c.start()
        second.append(c)
    cgrad[...] = dot_nt(gpe[E:, :], ef[2 * L:, :]).astype(BF16)
    for b in range(E // 128):
        backward(128 * b, 128)
    egrad[...] = dot_nt(gpe[0:E, :], ef[2 * L:, :]).astype(BF16)
    rsum = dot_tn(oh[...], gpe[...]).astype(BF16)
    base = base + dot_nt(rsum, ef[0:L, :])
    ssum = dot_tn(oh2[0:E, :], gpe[0:E, :])
    for c in second:
        c.wait_recv()
    ssum = (ssum + dot_tn(ohb, in_sums[0:R * S, :])).astype(BF16)
    grad[...] = (base + dot_nt(ssum, ef[L:2 * L, :])).astype(BF16)
    for c in first + second:
        c.wait_send()


def write_out(a, b, c, e, a_h, b_h, c_h, e_h, sem):
    copies = [
        pltpu.make_async_copy(src, dst, sem.at[i])
        for i, (src, dst) in enumerate(((a, a_h), (b, b_h), (c, c_h), (e, e_h)))
    ]
    for copy in copies:
        copy.start()
    for copy in copies:
        copy.wait()


def shards(
    node_latent, edge_latent, cut_latent, node_cotangent, edge_sender, edge_receiver, boundary_rows,
    cut_slot, cut_receiver, node_count, edge_count, edge_first, edge_second, edge_gain, node_first,
    node_second, node_gain,
):
    i32 = jnp.int32
    anyspec = pl.BlockSpec(memory_space=pl.ANY)
    outs = pl.pallas_call(
        kernel,
        out_shape=tuple(pltpu.VMEM((n, L), BF16) for n in (N, N, E, CUTS)),
        in_specs=[anyspec] * 17,
        out_specs=(pl.BlockSpec(memory_space=pltpu.VMEM),) * 4,
        scratch_shapes=[
            pltpu.VMEM((N, L), BF16), pltpu.VMEM((E, L), BF16), pltpu.VMEM((CUTS, L), BF16),
            pltpu.VMEM((N, L), BF16), pltpu.VMEM((1, E), i32), pltpu.VMEM((1, E), i32),
            pltpu.VMEM((R, 1, S), i32), pltpu.VMEM((R, 1, C), i32), pltpu.VMEM((R, 1, C), i32),
            pltpu.VMEM((1, 1), i32), pltpu.VMEM((1, 1), i32),
            pltpu.VMEM((3 * L, L), BF16), pltpu.VMEM((L, L), BF16), pltpu.VMEM((1, L), F32),
            pltpu.VMEM((2 * L, L), BF16), pltpu.VMEM((L, L), BF16), pltpu.VMEM((1, L), F32),
            pltpu.VMEM((R * S, L), BF16), pltpu.VMEM((N, L), BF16),
            pltpu.VMEM((N, L), BF16), pltpu.VMEM((N, L), BF16),
            pltpu.VMEM((2 * N, L), BF16), pltpu.VMEM((2 * N, L), BF16),
            pltpu.VMEM((ROWS, N), BF16), pltpu.VMEM((ROWS, N), BF16),
            pltpu.VMEM((ROWS, L), BF16), pltpu.VMEM((ROWS, 1), F32), pltpu.VMEM((ROWS, L), F32),
            pltpu.VMEM((ROWS, L), BF16),
            pltpu.SemaphoreType.DMA((17,)),
            pltpu.SemaphoreType.DMA((R,)), pltpu.SemaphoreType.DMA((R,)),
            pltpu.SemaphoreType.DMA((R,)), pltpu.SemaphoreType.DMA((R,)),
        ],
        compiler_params=pltpu.CompilerParams(collective_id=0, has_side_effects=True),
        name="message_step",
    )(
        node_latent[0], edge_latent[0], cut_latent[0].reshape(CUTS, L), node_cotangent[0],
        edge_sender, edge_receiver, boundary_rows.reshape(R, 1, S), cut_slot.reshape(R, 1, C), cut_receiver.reshape(R, 1, C),
        node_count.reshape(1, 1), edge_count.reshape(1, 1),
        edge_first, edge_second, edge_gain.reshape(1, L), node_first, node_second,
        node_gain.reshape(1, L),
    )
    updated, gradient, edge_gradient, cut_gradient = pl.pallas_call(
        write_out,
        out_shape=tuple(jax.ShapeDtypeStruct((n, L), BF16) for n in (N, N, E, CUTS)),
        in_specs=[pl.BlockSpec(memory_space=pltpu.VMEM)] * 4,
        out_specs=(anyspec,) * 4,
        scratch_shapes=[pltpu.SemaphoreType.DMA((4,))],
        name="write_out",
    )(*(pltpu.with_memory_space_constraint(o, pltpu.VMEM) for o in outs))
    return updated[None], gradient[None], edge_gradient[None], cut_gradient.reshape(1, R, C, L)


def solution(mesh):
    part = ("grp", "dev")
    three = P(part, None, None)
    four = P(part, None, None, None)
    placed = (
        three, three, four, three, P(part, None), P(part, None), three, three, three, P(part),
        P(part), P(), P(), P(), P(), P(), P(),
    )
    return jax.shard_map(
        shards, mesh=mesh, in_specs=placed, out_specs=(three, three, three, four), check_vma=False,
    )
```

```python
import jax
import jax.numpy as jnp
from jax import lax
from jax.experimental import pallas as pl
from jax.experimental.pallas import tpu as pltpu
from jax.sharding import PartitionSpec as P

F32 = jnp.float32
BF16 = jnp.bfloat16
MESH = pl.DeviceIdType.MESH
EPS = 1e-5

N = 128
L = 256
E = 384
R = 5
C = 64
S = 16
CUTS = R * C
ROWS = E + CUTS


def dot(a, b):
    return jnp.dot(a, b, preferred_element_type=F32)


def dot_nt(a, b):
    return lax.dot_general(a, b, (((1,), (1,)), ((), ())), preferred_element_type=F32)


def flip(index, bit):
    step = 1 << bit
    return index + step - 2 * step * lax.rem(lax.div(index, step), 2)


def column(rows_of, count, width):
    wide = jnp.concatenate([jnp.broadcast_to(rows_of(i), (width, width)) for i in range(count)], 0)
    total = count * width
    at = lax.broadcasted_iota(jnp.int32, (total, width), 0)
    lane = lax.broadcasted_iota(jnp.int32, (total, width), 1)
    keep = lax.rem(at, width) == lane
    return jnp.sum(jnp.where(keep, wide.astype(F32), 0.0), axis=1, keepdims=True)


def one_hot(col, width=N):
    lane = lax.broadcasted_iota(jnp.int32, (col.shape[0], width), 1).astype(F32)
    return (col == lane).astype(F32).astype(BF16)


def one_hot_t(row):
    at = lax.broadcasted_iota(jnp.int32, (N, row.shape[1]), 0)
    return (at == row).astype(F32).astype(BF16)


def silu_pair(half):
    t = jnp.tanh(half)
    act = half + half * t
    return act, (1.0 + t) + act * (1.0 - t)


def twice(a):
    return jnp.concatenate([a, a], 1)


def row_means(w):
    mean = dot_nt(jnp.full((N, L), 1.0 / L, BF16), w)
    high = mean.astype(BF16)
    return jnp.concatenate([high, (mean - high.astype(F32)).astype(BF16)], 1)


def centred(act, w, means):
    return dot(act, w) - twice(dot_nt(twice(act), means))


def total_of(a):
    return jnp.sum(a, axis=-1, keepdims=True)


def kernel(
    nodes_h, edges_h, cut_h, cot_h, send_h, recv_h, bound_h, slot_h, crecv_h, ncount_h, ecount_h,
    ef_h, es_h, eg_h, nf_h, ns_h, ng_h,
    upd, grad, egrad, cgrad,
    nodes, edges, cut, cot, sendi, recvi, bound, slot, crecv, ncount, ecount,
    ef, es, eg, nf, ns, ng,
    out_rows, in_rows, out_sums, in_sums, comb, weh, oht, pick, part, xb, side, slope, gpe,
    in_sem, s1, r1, s2, r2,
):
    loads = {}

    def load(key, src, dst):
        c = pltpu.make_async_copy(src, dst, in_sem.at[len(loads)])
        c.start()
        loads[key] = c

    def need(*keys):
        for k in keys:
            loads[k].wait()

    load("nodes", nodes_h, nodes)
    load("bound", bound_h, bound)
    g = lax.axis_index("grp")
    d = lax.axis_index("dev")
    partners = [
        (flip(g, 0), d), (flip(g, 1), d), (g, flip(d, 0)), (g, flip(d, 1)), (g, flip(d, 2)),
    ]
    barrier = pltpu.get_barrier_semaphore()
    for p in partners[::-1]:
        pl.semaphore_signal(barrier, inc=1, device_id=p, device_id_type=MESH)
    load("recv", recv_h, recvi)
    load("send", send_h, sendi)
    load("ecount", ecount_h, ecount)
    load("ef", ef_h, ef)
    load("edges", edges_h, edges)
    load("es", es_h, es)
    load("crecv", crecv_h, crecv)
    load("slot", slot_h, slot)
    load("cut", cut_h, cut)
    load("eg", eg_h, eg)
    load("nf", nf_h, nf)
    load("ns", ns_h, ns)
    load("ng", ng_h, ng)
    load("cot", cot_h, cot)
    load("ncount", ncount_h, ncount)

    eye = one_hot_t(lax.broadcasted_iota(jnp.int32, (1, N), 1))

    need("nodes", "bound")
    ohb = one_hot(column(lambda i: bound[i], R, S))
    out_rows[...] = dot(ohb, nodes[...]).astype(BF16)
    pl.semaphore_wait(barrier, R)

    def exchange(src, dst, send_sem, recv_sem):
        copies = []
        for r in (3, 1, 2, 4, 0):
            at = pl.ds(S * r, S)
            c = pltpu.make_async_remote_copy(
                src_ref=src.at[at], dst_ref=dst.at[at], send_sem=send_sem.at[r],
                recv_sem=recv_sem.at[r], device_id=partners[r], device_id_type=MESH)
            c.start()
            copies.append(c)
        return copies

    first = exchange(out_rows, in_rows, s1, r1)

    def tables(start, size):
        for b in range(start, start + size, N):
            n = min(N, start + size - b)
            pick[b:b + n, :] = dot_nt(eye[:n, :n], oht[:, b:b + n]).astype(BF16)

    def forward(start, half):
        size = half.shape[0]
        rows = pl.ds(start, size)
        act, sl = silu_pair(half)
        cent = centred(act.astype(BF16), es[...], edge_means)
        inv = lax.rsqrt(total_of(cent * cent) * (1.0 / L) + EPS)
        xh = (cent * inv).astype(BF16)
        xb[rows, :] = xh
        slope[rows, :] = sl * inv
        return dot(oht[0:N, start:start + size], xh)

    need("recv", "send", "ecount")
    lane = lax.broadcasted_iota(jnp.int32, (1, E), 1)
    oht[0:N, 0:E] = one_hot_t(jnp.where(lane < ecount[...], recvi[...], -1))
    oht[N:, 0:E] = one_hot_t(sendi[...])
    tables(0, E)
    need("ef")
    sender = ef[L:2 * L, :]
    weh[...] = (ef[2 * L:, :].astype(F32) * 0.5).astype(BF16)
    comb[0:N, :] = (dot(nodes[...], ef[0:L, :]) * 0.5).astype(BF16)
    comb[N:, :] = (dot(nodes[...], sender) * 0.5).astype(BF16)
    need("edges", "es")
    edge_means = row_means(es[...])
    total = forward(0, dot(pick[0:E, :], comb[...]) + dot(edges[...], weh[...]))

    need("crecv", "slot", "cut", "eg", "nf", "ns", "ng", "cot", "ncount")
    oht[0:N, E:] = one_hot_t(jnp.concatenate([crecv[r] for r in range(R)], 1))
    oht[N:, E:] = one_hot_t(jnp.concatenate([slot[r] + S * r for r in range(R)], 1))
    tables(E, CUTS)
    part[...] = dot(pick[E:, 0:N], comb[0:N, :]) + dot(cut[...], weh[...])
    ohtb = one_hot_t(jnp.concatenate([bound[r] for r in range(R)], 1))
    node_means = row_means(ns[...])
    pre_node_own = dot(nodes[...], nf[0:L, :])
    es_f = es[...].astype(F32)
    es_c = ((es_f - total_of(es_f) * (1.0 / L)) * (0.5 * eg[...])).astype(BF16)
    chain = dot(es_c, nf[L:, :]).astype(BF16)
    live = lax.broadcasted_iota(jnp.int32, (N, 1), 0) < ncount[...]
    gain = ng[...]
    mcot = jnp.where(live, cot[...].astype(F32), 0.0)
    dc = mcot * gain
    dc = dc - total_of(dc) * (1.0 / L)

    for c in first:
        c.wait_recv()
    arrived = (dot(in_rows[...], sender) * 0.5).astype(BF16)
    arrived = jnp.concatenate([arrived, jnp.zeros((N - R * S, L), BF16)], 0)
    total = total + forward(E, part[...] + dot(pick[E:, N:], arrived))

    received = (total * eg[...]).astype(BF16)
    act, sl = silu_pair(0.5 * (pre_node_own + dot(received, nf[L:, :])))
    cent = centred(act.astype(BF16), ns[...], node_means)
    along = total_of(dc * cent) * (1.0 / L)
    ninv = lax.rsqrt(total_of(cent * cent) * (1.0 / L) + EPS)
    goo = (ninv * dc - cent * (ninv * ninv * ninv * along)).astype(BF16)
    gpn = (dot_nt(goo, ns[...]) * (0.5 * sl)).astype(BF16)
    gm = (dot_nt(gpn, nf[L:, :]) * (0.5 * eg[...])).astype(BF16)
    gm2 = dot_nt(gpn, chain).astype(BF16)

    def backward(start, size):
        rows = pl.ds(start, size)
        to = pick[rows, 0:N]
        m2 = total_of(dot_nt(xb[rows, :], gm) * to.astype(F32)) * (1.0 / L)
        gpe[rows, :] = ((dot(to, gm2) - m2 * side[rows, :]) * slope[rows, :]).astype(BF16)

    side[E:, :] = dot_nt(xb[E:, :], es[...])
    backward(E, CUTS)
    out_sums[...] = dot(oht[N:N + R * S, E:], gpe[E:, :]).astype(BF16)
    second = exchange(out_sums, in_sums, s2, r2)

    upd[...] = jnp.where(live, nodes[...].astype(F32) + cent * ninv * gain, 0.0).astype(BF16)
    base = mcot + dot_nt(gpn, nf[0:L, :])
    latent_t = ef[2 * L:, :]
    cgrad[...] = dot_nt(gpe[E:, :], latent_t).astype(BF16)
    side[0:E, :] = dot_nt(xb[0:E, :], es[...])
    backward(0, E)
    egrad[...] = dot_nt(gpe[0:E, :], latent_t).astype(BF16)
    rsum = dot(oht[0:N, :], gpe[...]).astype(BF16)
    base = base + dot_nt(rsum, ef[0:L, :])
    ssum = dot(oht[N:, 0:E], gpe[0:E, :])
    for c in second:
        c.wait_recv()
    ssum = (ssum + dot(ohtb, in_sums[...])).astype(BF16)
    grad[...] = (base + dot_nt(ssum, sender)).astype(BF16)
    for c in first + second:
        c.wait_send()


def write_out(a, b, c, e, a_h, b_h, c_h, e_h, sem):
    copies = [
        pltpu.make_async_copy(src, dst, sem.at[i])
        for i, (src, dst) in enumerate(((a, a_h), (b, b_h), (c, c_h), (e, e_h)))
    ]
    for copy in copies:
        copy.start()
    for copy in copies:
        copy.wait()


def shards(
    node_latent, edge_latent, cut_latent, node_cotangent, edge_sender, edge_receiver, boundary_rows,
    cut_slot, cut_receiver, node_count, edge_count, edge_first, edge_second, edge_gain, node_first,
    node_second, node_gain,
):
    i32 = jnp.int32
    anyspec = pl.BlockSpec(memory_space=pl.ANY)
    outs = pl.pallas_call(
        kernel,
        out_shape=tuple(pltpu.VMEM((n, L), BF16) for n in (N, N, E, CUTS)),
        in_specs=[anyspec] * 17,
        out_specs=(pl.BlockSpec(memory_space=pltpu.VMEM),) * 4,
        scratch_shapes=[
            pltpu.VMEM((N, L), BF16), pltpu.VMEM((E, L), BF16), pltpu.VMEM((CUTS, L), BF16),
            pltpu.VMEM((N, L), BF16), pltpu.VMEM((1, E), i32), pltpu.VMEM((1, E), i32),
            pltpu.VMEM((R, 1, S), i32), pltpu.VMEM((R, 1, C), i32), pltpu.VMEM((R, 1, C), i32),
            pltpu.VMEM((1, 1), i32), pltpu.VMEM((1, 1), i32),
            pltpu.VMEM((3 * L, L), BF16), pltpu.VMEM((L, L), BF16), pltpu.VMEM((1, L), F32),
            pltpu.VMEM((2 * L, L), BF16), pltpu.VMEM((L, L), BF16), pltpu.VMEM((1, L), F32),
            pltpu.VMEM((R * S, L), BF16), pltpu.VMEM((R * S, L), BF16),
            pltpu.VMEM((R * S, L), BF16), pltpu.VMEM((R * S, L), BF16),
            pltpu.VMEM((2 * N, L), BF16), pltpu.VMEM((L, L), BF16),
            pltpu.VMEM((2 * N, ROWS), BF16), pltpu.VMEM((ROWS, 2 * N), BF16),
            pltpu.VMEM((CUTS, L), F32), pltpu.VMEM((ROWS, L), BF16), pltpu.VMEM((ROWS, L), F32),
            pltpu.VMEM((ROWS, L), F32), pltpu.VMEM((ROWS, L), BF16),
            pltpu.SemaphoreType.DMA((17,)),
            pltpu.SemaphoreType.DMA((R,)), pltpu.SemaphoreType.DMA((R,)),
            pltpu.SemaphoreType.DMA((R,)), pltpu.SemaphoreType.DMA((R,)),
        ],
        compiler_params=pltpu.CompilerParams(collective_id=0, has_side_effects=True),
        name="message_step",
    )(
        node_latent[0], edge_latent[0], cut_latent[0].reshape(CUTS, L), node_cotangent[0],
        edge_sender, edge_receiver, boundary_rows.reshape(R, 1, S), cut_slot.reshape(R, 1, C), cut_receiver.reshape(R, 1, C),
        node_count.reshape(1, 1), edge_count.reshape(1, 1),
        edge_first, edge_second, edge_gain.reshape(1, L), node_first, node_second,
        node_gain.reshape(1, L),
    )
    updated, gradient, edge_gradient, cut_gradient = pl.pallas_call(
        write_out,
        out_shape=tuple(jax.ShapeDtypeStruct((n, L), BF16) for n in (N, N, E, CUTS)),
        in_specs=[pl.BlockSpec(memory_space=pltpu.VMEM)] * 4,
        out_specs=(anyspec,) * 4,
        scratch_shapes=[pltpu.SemaphoreType.DMA((4,))],
        name="write_out",
    )(*(pltpu.with_memory_space_constraint(o, pltpu.VMEM) for o in outs))
    return updated[None], gradient[None], edge_gradient[None], cut_gradient.reshape(1, R, C, L)


def solution(mesh):
    part = ("grp", "dev")
    three = P(part, None, None)
    four = P(part, None, None, None)
    placed = (
        three, three, four, three, P(part, None), P(part, None), three, three, three, P(part),
        P(part), P(), P(), P(), P(), P(), P(),
    )
    return jax.shard_map(
        shards, mesh=mesh, in_specs=placed, out_specs=(three, three, three, four), check_vma=False,
    )
```

```python
import jax
import jax.numpy as jnp
from jax import lax
from jax.experimental import pallas as pl
from jax.experimental.pallas import tpu as pltpu
from jax.sharding import PartitionSpec as P

F32 = jnp.float32
BF16 = jnp.bfloat16
MESH = pl.DeviceIdType.MESH
EPS = 1e-5

N = 128
L = 256
E = 384
R = 5
C = 64
S = 16
CUTS = R * C
ROWS = E + CUTS


def dot(a, b):
    return jnp.dot(a, b, preferred_element_type=F32)


def dot_nt(a, b):
    return lax.dot_general(a, b, (((1,), (1,)), ((), ())), preferred_element_type=F32)


def flip(index, bit):
    step = 1 << bit
    return index + step - 2 * step * lax.rem(lax.div(index, step), 2)


def column(rows_of, count, width):
    wide = jnp.concatenate([jnp.broadcast_to(rows_of(i), (width, width)) for i in range(count)], 0)
    total = count * width
    at = lax.broadcasted_iota(jnp.int32, (total, width), 0)
    lane = lax.broadcasted_iota(jnp.int32, (total, width), 1)
    keep = lax.rem(at, width) == lane
    return jnp.sum(jnp.where(keep, wide.astype(F32), 0.0), axis=1, keepdims=True)


def one_hot(col, width=N):
    lane = lax.broadcasted_iota(jnp.int32, (col.shape[0], width), 1).astype(F32)
    return (col == lane).astype(F32).astype(BF16)


def one_hot_t(row):
    at = lax.broadcasted_iota(jnp.int32, (N, row.shape[1]), 0)
    return (at == row).astype(F32).astype(BF16)


def silu_pair(half):
    t = jnp.tanh(half)
    act = half + half * t
    return act, (1.0 + t) + act * (1.0 - t)


def total_of(a):
    return jnp.sum(a, axis=-1, keepdims=True)


def kernel(
    nodes_h, edges_h, cut_h, cot_h, send_h, recv_h, bound_h, slot_h, crecv_h, ncount_h, ecount_h,
    ef_h, es_h, eg_h, nf_h, ns_h, ng_h,
    upd, grad, egrad, cgrad,
    nodes, edges, cut, cot, sendi, recvi, bound, slot, crecv,
    ef, es, eg, nf, ns, ng,
    out_rows, in_rows, out_sums, in_sums, comb, weh, oht, pick, part, xb, side, slope, gpe,
    in_sem, s1, r1, s2, r2,
):
    loads = {}

    def load(key, src, dst):
        c = pltpu.make_async_copy(src, dst, in_sem.at[len(loads)])
        c.start()
        loads[key] = c

    def need(*keys):
        for k in keys:
            loads[k].wait()

    load("nodes", nodes_h, nodes)
    load("bound", bound_h, bound)
    g = lax.axis_index("grp")
    d = lax.axis_index("dev")
    partners = [
        (flip(g, 0), d), (flip(g, 1), d), (g, flip(d, 0)), (g, flip(d, 1)), (g, flip(d, 2)),
    ]
    barrier = pltpu.get_barrier_semaphore()
    for p in partners[::-1]:
        pl.semaphore_signal(barrier, inc=1, device_id=p, device_id_type=MESH)
    load("recv", recv_h, recvi)
    load("send", send_h, sendi)
    load("ef", ef_h, ef)
    load("edges", edges_h, edges)
    load("es", es_h, es)
    load("crecv", crecv_h, crecv)
    load("slot", slot_h, slot)
    load("cut", cut_h, cut)
    load("eg", eg_h, eg)
    load("nf", nf_h, nf)
    load("ns", ns_h, ns)
    load("ng", ng_h, ng)
    load("cot", cot_h, cot)

    eye = one_hot_t(lax.broadcasted_iota(jnp.int32, (1, N), 1))

    need("nodes", "bound")
    ohb = one_hot(column(lambda i: bound[i], R, S))
    out_rows[...] = dot(ohb, nodes[...]).astype(BF16)
    pl.semaphore_wait(barrier, R)

    def exchange(src, dst, send_sem, recv_sem):
        copies = []
        for r in (3, 1, 2, 4, 0):
            at = pl.ds(S * r, S)
            c = pltpu.make_async_remote_copy(
                src_ref=src.at[at], dst_ref=dst.at[at], send_sem=send_sem.at[r],
                recv_sem=recv_sem.at[r], device_id=partners[r], device_id_type=MESH)
            c.start()
            copies.append(c)
        return copies

    first = exchange(out_rows, in_rows, s1, r1)

    def tables(start, size):
        for b in range(start, start + size, N):
            n = min(N, start + size - b)
            pick[b:b + n, :] = dot_nt(eye[:n, :n], oht[:, b:b + n]).astype(BF16)

    def forward(start, half):
        size = half.shape[0]
        rows = pl.ds(start, size)
        act, sl = silu_pair(half)
        cent = dot(act.astype(BF16), es[...])
        cent = cent - total_of(cent) * (1.0 / L)
        inv = lax.rsqrt(total_of(cent * cent) * (1.0 / L) + EPS)
        xh = (cent * inv).astype(BF16)
        xb[rows, :] = xh
        slope[rows, :] = sl * inv
        return dot(oht[0:N, start:start + size], xh)

    need("recv", "send")
    lane = lax.broadcasted_iota(jnp.int32, (1, E), 1)
    oht[0:N, 0:E] = one_hot_t(jnp.where(lane < ecount_h[0, 0], recvi[...], -1))
    oht[N:, 0:E] = one_hot_t(sendi[...])
    tables(0, E)
    need("ef")
    sender = ef[L:2 * L, :]
    weh[...] = (ef[2 * L:, :].astype(F32) * 0.5).astype(BF16)
    comb[0:N, :] = (dot(nodes[...], ef[0:L, :]) * 0.5).astype(BF16)
    comb[N:, :] = (dot(nodes[...], sender) * 0.5).astype(BF16)
    need("edges", "es")
    total = forward(0, dot(pick[0:E, :], comb[...]) + dot(edges[...], weh[...]))

    need("crecv", "slot", "cut", "eg", "nf", "ns", "ng", "cot")
    oht[0:N, E:] = one_hot_t(jnp.concatenate([crecv[r] for r in range(R)], 1))
    oht[N:, E:] = one_hot_t(jnp.concatenate([slot[r] + S * r for r in range(R)], 1))
    tables(E, CUTS)
    part[...] = dot(pick[E:, 0:N], comb[0:N, :]) + dot(cut[...], weh[...])
    ohtb = one_hot_t(jnp.concatenate([bound[r] for r in range(R)], 1))
    pre_node_own = dot(nodes[...], nf[0:L, :])
    es_f = es[...].astype(F32)
    es_c = ((es_f - total_of(es_f) * (1.0 / L)) * (0.5 * eg[...])).astype(BF16)
    chain = dot(es_c, nf[L:, :]).astype(BF16)
    live = lax.broadcasted_iota(jnp.int32, (N, 1), 0) < ncount_h[0, 0]
    gain = ng[...]
    mcot = jnp.where(live, cot[...].astype(F32), 0.0)
    dc = mcot * gain
    dc = dc - total_of(dc) * (1.0 / L)

    for c in first:
        c.wait_recv()
    arrived = (dot(in_rows[...], sender) * 0.5).astype(BF16)
    arrived = jnp.concatenate([arrived, jnp.zeros((N - R * S, L), BF16)], 0)
    total = total + forward(E, part[...] + dot(pick[E:, N:], arrived))

    received = (total * eg[...]).astype(BF16)
    side[E:, :] = dot_nt(xb[E:, :], es[...])
    act, sl = silu_pair(0.5 * (pre_node_own + dot(received, nf[L:, :])))
    cent = dot(act.astype(BF16), ns[...])
    cent = cent - total_of(cent) * (1.0 / L)
    along = total_of(dc * cent) * (1.0 / L)
    ninv = lax.rsqrt(total_of(cent * cent) * (1.0 / L) + EPS)
    goo = (ninv * dc - cent * (ninv * ninv * ninv * along)).astype(BF16)
    gpn = (dot_nt(goo, ns[...]) * (0.5 * sl)).astype(BF16)
    gm = (dot_nt(gpn, nf[L:, :]) * (0.5 * eg[...])).astype(BF16)
    gm2 = dot_nt(gpn, chain).astype(BF16)

    def backward(start, size):
        rows = pl.ds(start, size)
        to = pick[rows, 0:N]
        m2 = total_of(dot_nt(xb[rows, :], gm) * to.astype(F32)) * (1.0 / L)
        gpe[rows, :] = ((dot(to, gm2) - m2 * side[rows, :]) * slope[rows, :]).astype(BF16)

    backward(E, CUTS)
    out_sums[...] = dot(oht[N:N + R * S, E:], gpe[E:, :]).astype(BF16)
    second = exchange(out_sums, in_sums, s2, r2)

    upd[...] = jnp.where(live, nodes[...].astype(F32) + cent * ninv * gain, 0.0).astype(BF16)
    base = mcot + dot_nt(gpn, nf[0:L, :])
    latent_t = ef[2 * L:, :]
    cgrad[...] = dot_nt(gpe[E:, :], latent_t).astype(BF16)
    side[0:E, :] = dot_nt(xb[0:E, :], es[...])
    backward(0, E)
    egrad[...] = dot_nt(gpe[0:E, :], latent_t).astype(BF16)
    rsum = dot(oht[0:N, :], gpe[...]).astype(BF16)
    base = base + dot_nt(rsum, ef[0:L, :])
    ssum = dot(oht[N:, 0:E], gpe[0:E, :])
    for c in second:
        c.wait_recv()
    ssum = (ssum + dot(ohtb, in_sums[...])).astype(BF16)
    grad[...] = (base + dot_nt(ssum, sender)).astype(BF16)
    for c in first + second:
        c.wait_send()


def write_out(a, b, c, e, a_h, b_h, c_h, e_h, sem):
    copies = [
        pltpu.make_async_copy(src, dst, sem.at[i])
        for i, (src, dst) in enumerate(((a, a_h), (b, b_h), (c, c_h), (e, e_h)))
    ]
    for copy in copies:
        copy.start()
    for copy in copies:
        copy.wait()


def shards(
    node_latent, edge_latent, cut_latent, node_cotangent, edge_sender, edge_receiver, boundary_rows,
    cut_slot, cut_receiver, node_count, edge_count, edge_first, edge_second, edge_gain, node_first,
    node_second, node_gain,
):
    i32 = jnp.int32
    anyspec = pl.BlockSpec(memory_space=pl.ANY)
    outs = pl.pallas_call(
        kernel,
        out_shape=tuple(pltpu.VMEM((n, L), BF16) for n in (N, N, E, CUTS)),
        in_specs=[anyspec] * 9 + [pl.BlockSpec(memory_space=pltpu.SMEM)] * 2 + [anyspec] * 6,
        out_specs=(pl.BlockSpec(memory_space=pltpu.VMEM),) * 4,
        scratch_shapes=[
            pltpu.VMEM((N, L), BF16), pltpu.VMEM((E, L), BF16), pltpu.VMEM((CUTS, L), BF16),
            pltpu.VMEM((N, L), BF16), pltpu.VMEM((1, E), i32), pltpu.VMEM((1, E), i32),
            pltpu.VMEM((R, 1, S), i32), pltpu.VMEM((R, 1, C), i32), pltpu.VMEM((R, 1, C), i32),
            pltpu.VMEM((3 * L, L), BF16), pltpu.VMEM((L, L), BF16), pltpu.VMEM((1, L), F32),
            pltpu.VMEM((2 * L, L), BF16), pltpu.VMEM((L, L), BF16), pltpu.VMEM((1, L), F32),
            pltpu.VMEM((R * S, L), BF16), pltpu.VMEM((R * S, L), BF16),
            pltpu.VMEM((R * S, L), BF16), pltpu.VMEM((R * S, L), BF16),
            pltpu.VMEM((2 * N, L), BF16), pltpu.VMEM((L, L), BF16),
            pltpu.VMEM((2 * N, ROWS), BF16), pltpu.VMEM((ROWS, 2 * N), BF16),
            pltpu.VMEM((CUTS, L), F32), pltpu.VMEM((ROWS, L), BF16), pltpu.VMEM((ROWS, L), F32),
            pltpu.VMEM((ROWS, L), F32), pltpu.VMEM((ROWS, L), BF16),
            pltpu.SemaphoreType.DMA((15,)),
            pltpu.SemaphoreType.DMA((R,)), pltpu.SemaphoreType.DMA((R,)),
            pltpu.SemaphoreType.DMA((R,)), pltpu.SemaphoreType.DMA((R,)),
        ],
        compiler_params=pltpu.CompilerParams(collective_id=0, has_side_effects=True),
        name="message_step",
    )(
        node_latent[0], edge_latent[0], cut_latent[0].reshape(CUTS, L), node_cotangent[0],
        edge_sender, edge_receiver, boundary_rows.reshape(R, 1, S), cut_slot.reshape(R, 1, C), cut_receiver.reshape(R, 1, C),
        node_count.reshape(1, 1), edge_count.reshape(1, 1),
        edge_first, edge_second, edge_gain.reshape(1, L), node_first, node_second,
        node_gain.reshape(1, L),
    )
    updated, gradient, edge_gradient, cut_gradient = pl.pallas_call(
        write_out,
        out_shape=tuple(jax.ShapeDtypeStruct((n, L), BF16) for n in (N, N, E, CUTS)),
        in_specs=[pl.BlockSpec(memory_space=pltpu.VMEM)] * 4,
        out_specs=(anyspec,) * 4,
        scratch_shapes=[pltpu.SemaphoreType.DMA((4,))],
        name="write_out",
    )(*(pltpu.with_memory_space_constraint(o, pltpu.VMEM) for o in outs))
    return updated[None], gradient[None], edge_gradient[None], cut_gradient.reshape(1, R, C, L)


def solution(mesh):
    part = ("grp", "dev")
    three = P(part, None, None)
    four = P(part, None, None, None)
    placed = (
        three, three, four, three, P(part, None), P(part, None), three, three, three, P(part),
        P(part), P(), P(), P(), P(), P(), P(),
    )
    return jax.shard_map(
        shards, mesh=mesh, in_specs=placed, out_specs=(three, three, three, four), check_vma=False,
    )
```

```python
import jax
import jax.numpy as jnp
from jax import lax
from jax.experimental import pallas as pl
from jax.experimental.pallas import tpu as pltpu
from jax.sharding import PartitionSpec as P

F32 = jnp.float32
BF16 = jnp.bfloat16
MESH = pl.DeviceIdType.MESH
EPS = 1e-5

N = 128
L = 256
E = 384
R = 5
C = 64
S = 16
CUTS = R * C
ROWS = E + CUTS


def dot(a, b):
    return jnp.dot(a, b, preferred_element_type=F32)


def dot_nt(a, b):
    return lax.dot_general(a, b, (((1,), (1,)), ((), ())), preferred_element_type=F32)


def flip(index, bit):
    step = 1 << bit
    return index + step - 2 * step * lax.rem(lax.div(index, step), 2)


def column(rows_of, count, width):
    wide = jnp.concatenate([jnp.broadcast_to(rows_of(i), (width, width)) for i in range(count)], 0)
    total = count * width
    at = lax.broadcasted_iota(jnp.int32, (total, width), 0)
    lane = lax.broadcasted_iota(jnp.int32, (total, width), 1)
    keep = lax.rem(at, width) == lane
    return jnp.sum(jnp.where(keep, wide.astype(F32), 0.0), axis=1, keepdims=True)


def one_hot(col, width=N):
    lane = lax.broadcasted_iota(jnp.int32, (col.shape[0], width), 1).astype(F32)
    return (col == lane).astype(F32).astype(BF16)


def one_hot_t(row):
    at = lax.broadcasted_iota(jnp.int32, (N, row.shape[1]), 0)
    return (at == row).astype(F32).astype(BF16)


def silu_pair(half):
    t = jnp.tanh(half)
    act = half + half * t
    return act, (1.0 + t) + act * (1.0 - t)


def total_of(a):
    return jnp.sum(a, axis=-1, keepdims=True)


def kernel(
    nodes_h, edges_h, cut_h, cot_h, send_h, recv_h, bound_h, slot_h, crecv_h, ncount_h, ecount_h,
    ef_h, es_h, eg_h, nf_h, ns_h, ng_h,
    upd, grad, egrad, cgrad,
    nodes, edges, cut, cot, sendi, recvi, bound, slot, crecv,
    ef, es, eg, nf, ns, ng,
    out_rows, in_rows, out_sums, in_sums, comb, weh, oht, pick, part, xb, side, slope, gpe,
    in_sem, s1, r1, s2, r2,
):
    loads = {}

    def load(key, src, dst):
        c = pltpu.make_async_copy(src, dst, in_sem.at[len(loads)])
        c.start()
        loads[key] = c

    def need(*keys):
        for k in keys:
            loads[k].wait()

    load("nodes", nodes_h, nodes)
    load("bound", bound_h, bound)
    g = lax.axis_index("grp")
    d = lax.axis_index("dev")
    partners = [
        (flip(g, 0), d), (flip(g, 1), d), (g, flip(d, 0)), (g, flip(d, 1)), (g, flip(d, 2)),
    ]
    barrier = pltpu.get_barrier_semaphore()
    for p in partners[::-1]:
        pl.semaphore_signal(barrier, inc=1, device_id=p, device_id_type=MESH)
    load("recv", recv_h, recvi)
    load("send", send_h, sendi)
    load("ef", ef_h, ef)
    load("edges", edges_h, edges)
    load("es", es_h, es)
    load("crecv", crecv_h, crecv)
    load("slot", slot_h, slot)
    load("cut", cut_h, cut)
    load("eg", eg_h, eg)
    load("nf", nf_h, nf)
    load("ns", ns_h, ns)
    load("ng", ng_h, ng)
    load("cot", cot_h, cot)

    need("nodes", "bound")
    ohb = one_hot(column(lambda i: bound[i], R, S))
    out_rows[...] = dot(ohb, nodes[...]).astype(BF16)
    pl.semaphore_wait(barrier, R)

    def exchange(src, dst, send_sem, recv_sem):
        copies = []
        for r in (3, 1, 2, 4, 0):
            at = pl.ds(S * r, S)
            c = pltpu.make_async_remote_copy(
                src_ref=src.at[at], dst_ref=dst.at[at], send_sem=send_sem.at[r],
                recv_sem=recv_sem.at[r], device_id=partners[r], device_id_type=MESH)
            c.start()
            copies.append(c)
        return copies

    first = exchange(out_rows, in_rows, s1, r1)

    def tables(start, size):
        for b in range(start, start + size, N):
            n = min(N, start + size - b)
            pick[b:b + n, :] = oht[:, b:b + n].T

    def forward(start, half):
        size = half.shape[0]
        rows = pl.ds(start, size)
        act, sl = silu_pair(half)
        cent = dot(act.astype(BF16), es[...])
        cent = cent - total_of(cent) * (1.0 / L)
        inv = lax.rsqrt(total_of(cent * cent) * (1.0 / L) + EPS)
        xh = (cent * inv).astype(BF16)
        xb[rows, :] = xh
        slope[rows, :] = sl * inv
        return dot(oht[0:N, start:start + size], xh)

    need("recv", "send")
    lane = lax.broadcasted_iota(jnp.int32, (1, E), 1)
    oht[0:N, 0:E] = one_hot_t(jnp.where(lane < ecount_h[0, 0], recvi[...], -1))
    oht[N:, 0:E] = one_hot_t(sendi[...])
    tables(0, E)
    need("ef")
    sender = ef[L:2 * L, :]
    weh[...] = (ef[2 * L:, :].astype(F32) * 0.5).astype(BF16)
    comb[0:N, :] = (dot(nodes[...], ef[0:L, :]) * 0.5).astype(BF16)
    comb[N:, :] = (dot(nodes[...], sender) * 0.5).astype(BF16)
    need("edges", "es")
    total = forward(0, dot(pick[0:E, :], comb[...]) + dot(edges[...], weh[...]))

    need("crecv", "slot", "cut", "eg", "nf", "ns", "ng", "cot")
    oht[0:N, E:] = one_hot_t(jnp.concatenate([crecv[r] for r in range(R)], 1))
    oht[N:, E:] = one_hot_t(jnp.concatenate([slot[r] + S * r for r in range(R)], 1))
    tables(E, CUTS)
    part[...] = dot(pick[E:, 0:N], comb[0:N, :]) + dot(cut[...], weh[...])
    ohtb = one_hot_t(jnp.concatenate([bound[r] for r in range(R)], 1))
    pre_node_own = dot(nodes[...], nf[0:L, :])
    es_f = es[...].astype(F32)
    es_c = ((es_f - total_of(es_f) * (1.0 / L)) * (0.5 * eg[...])).astype(BF16)
    chain = dot(es_c, nf[L:, :]).astype(BF16)
    live = lax.broadcasted_iota(jnp.int32, (N, 1), 0) < ncount_h[0, 0]
    gain = ng[...]
    mcot = jnp.where(live, cot[...].astype(F32), 0.0)
    dc = mcot * gain
    dc = dc - total_of(dc) * (1.0 / L)

    for c in first:
        c.wait_recv()
    arrived = (dot(in_rows[...], sender) * 0.5).astype(BF16)
    arrived = jnp.concatenate([arrived, jnp.zeros((N - R * S, L), BF16)], 0)
    total = total + forward(E, part[...] + dot(pick[E:, N:], arrived))

    received = (total * eg[...]).astype(BF16)
    side[E:, :] = dot_nt(xb[E:, :], es[...])
    act, sl = silu_pair(0.5 * (pre_node_own + dot(received, nf[L:, :])))
    cent = dot(act.astype(BF16), ns[...])
    cent = cent - total_of(cent) * (1.0 / L)
    along = total_of(dc * cent) * (1.0 / L)
    ninv = lax.rsqrt(total_of(cent * cent) * (1.0 / L) + EPS)
    goo = (ninv * dc - cent * (ninv * ninv * ninv * along)).astype(BF16)
    gpn = (dot_nt(goo, ns[...]) * (0.5 * sl)).astype(BF16)
    gm = (dot_nt(gpn, nf[L:, :]) * (0.5 * eg[...])).astype(BF16)
    gm2 = dot_nt(gpn, chain).astype(BF16)

    def backward(start, size):
        rows = pl.ds(start, size)
        to = pick[rows, 0:N]
        m2 = total_of(dot_nt(xb[rows, :], gm) * to.astype(F32)) * (1.0 / L)
        gpe[rows, :] = ((dot(to, gm2) - m2 * side[rows, :]) * slope[rows, :]).astype(BF16)

    backward(E, CUTS)
    out_sums[...] = dot(oht[N:N + R * S, E:], gpe[E:, :]).astype(BF16)
    second = exchange(out_sums, in_sums, s2, r2)

    upd[...] = jnp.where(live, nodes[...].astype(F32) + cent * ninv * gain, 0.0).astype(BF16)
    base = mcot + dot_nt(gpn, nf[0:L, :])
    latent_t = ef[2 * L:, :]
    cgrad[...] = dot_nt(gpe[E:, :], latent_t).astype(BF16)
    side[0:E, :] = dot_nt(xb[0:E, :], es[...])
    backward(0, E)
    egrad[...] = dot_nt(gpe[0:E, :], latent_t).astype(BF16)
    rsum = dot(oht[0:N, :], gpe[...]).astype(BF16)
    base = base + dot_nt(rsum, ef[0:L, :])
    ssum = dot(oht[N:, 0:E], gpe[0:E, :]).astype(BF16)
    base = base + dot_nt(ssum, sender)
    for c in second:
        c.wait_recv()
    back = dot_nt(in_sums[...], sender).astype(BF16)
    grad[...] = (base + dot(ohtb, back)).astype(BF16)
    for c in first + second:
        c.wait_send()


def write_out(a, b, c, e, a_h, b_h, c_h, e_h, sem):
    copies = [
        pltpu.make_async_copy(src, dst, sem.at[i])
        for i, (src, dst) in enumerate(((a, a_h), (b, b_h), (c, c_h), (e, e_h)))
    ]
    for copy in copies:
        copy.start()
    for copy in copies:
        copy.wait()


def shards(
    node_latent, edge_latent, cut_latent, node_cotangent, edge_sender, edge_receiver, boundary_rows,
    cut_slot, cut_receiver, node_count, edge_count, edge_first, edge_second, edge_gain, node_first,
    node_second, node_gain,
):
    i32 = jnp.int32
    anyspec = pl.BlockSpec(memory_space=pl.ANY)
    outs = pl.pallas_call(
        kernel,
        out_shape=tuple(pltpu.VMEM((n, L), BF16) for n in (N, N, E, CUTS)),
        in_specs=[anyspec] * 9 + [pl.BlockSpec(memory_space=pltpu.SMEM)] * 2 + [anyspec] * 6,
        out_specs=(pl.BlockSpec(memory_space=pltpu.VMEM),) * 4,
        scratch_shapes=[
            pltpu.VMEM((N, L), BF16), pltpu.VMEM((E, L), BF16), pltpu.VMEM((CUTS, L), BF16),
            pltpu.VMEM((N, L), BF16), pltpu.VMEM((1, E), i32), pltpu.VMEM((1, E), i32),
            pltpu.VMEM((R, 1, S), i32), pltpu.VMEM((R, 1, C), i32), pltpu.VMEM((R, 1, C), i32),
            pltpu.VMEM((3 * L, L), BF16), pltpu.VMEM((L, L), BF16), pltpu.VMEM((1, L), F32),
            pltpu.VMEM((2 * L, L), BF16), pltpu.VMEM((L, L), BF16), pltpu.VMEM((1, L), F32),
            pltpu.VMEM((R * S, L), BF16), pltpu.VMEM((R * S, L), BF16),
            pltpu.VMEM((R * S, L), BF16), pltpu.VMEM((R * S, L), BF16),
            pltpu.VMEM((2 * N, L), BF16), pltpu.VMEM((L, L), BF16),
            pltpu.VMEM((2 * N, ROWS), BF16), pltpu.VMEM((ROWS, 2 * N), BF16),
            pltpu.VMEM((CUTS, L), F32), pltpu.VMEM((ROWS, L), BF16), pltpu.VMEM((ROWS, L), F32),
            pltpu.VMEM((ROWS, L), F32), pltpu.VMEM((ROWS, L), BF16),
            pltpu.SemaphoreType.DMA((15,)),
            pltpu.SemaphoreType.DMA((R,)), pltpu.SemaphoreType.DMA((R,)),
            pltpu.SemaphoreType.DMA((R,)), pltpu.SemaphoreType.DMA((R,)),
        ],
        compiler_params=pltpu.CompilerParams(collective_id=0, has_side_effects=True),
        name="message_step",
    )(
        node_latent[0], edge_latent[0], cut_latent[0].reshape(CUTS, L), node_cotangent[0],
        edge_sender, edge_receiver, boundary_rows.reshape(R, 1, S), cut_slot.reshape(R, 1, C), cut_receiver.reshape(R, 1, C),
        node_count.reshape(1, 1), edge_count.reshape(1, 1),
        edge_first, edge_second, edge_gain.reshape(1, L), node_first, node_second,
        node_gain.reshape(1, L),
    )
    updated, gradient, edge_gradient, cut_gradient = pl.pallas_call(
        write_out,
        out_shape=tuple(jax.ShapeDtypeStruct((n, L), BF16) for n in (N, N, E, CUTS)),
        in_specs=[pl.BlockSpec(memory_space=pltpu.VMEM)] * 4,
        out_specs=(anyspec,) * 4,
        scratch_shapes=[pltpu.SemaphoreType.DMA((4,))],
        name="write_out",
    )(*(pltpu.with_memory_space_constraint(o, pltpu.VMEM) for o in outs))
    return updated[None], gradient[None], edge_gradient[None], cut_gradient.reshape(1, R, C, L)


def solution(mesh):
    part = ("grp", "dev")
    three = P(part, None, None)
    four = P(part, None, None, None)
    placed = (
        three, three, four, three, P(part, None), P(part, None), three, three, three, P(part),
        P(part), P(), P(), P(), P(), P(), P(),
    )
    return jax.shard_map(
        shards, mesh=mesh, in_specs=placed, out_specs=(three, three, three, four), check_vma=False,
    )
```
